32 devices in a mesh: grp: 2 (over y), row: 8 (over z, core), col: 2 (over x), ch: 1.
Axes of the slice: x: 2, y: 2, z: 4, core: 2. Of those that a mesh axis runs over, the one named last changes fastest.
Arguments:
- maps: bfloat16 [64, 512, 256], P('ch', ('grp', 'row'), 'col'), parts along dimension 1, may hold values from -6 to 6
- weights: bfloat16 [6, 3, 3, 64, 64], P(None, None, None, 'ch'), may hold values from -0.25 to 0.25
- biases: bfloat16 [6, 64], P(None, 'ch'), may hold values from -3 to 3
- dilations: int32 [6], replicated, may hold values from 1 to 8, as said below
Outputs:
- decoded: bfloat16 [64, 512, 256], P('ch', ('grp', 'row'), 'col'), parts along dimension 1
The draws below stay inside these ranges and needn't reach their ends.
There are 2 independent parts, one for each index of `grp`. The reference program is written for one: setup_inputs(seed, part) draws one part's arguments, and reference() takes and returns one part's arrays. A program takes and returns all parts, laid end to end along the dimension named above; an argument that names none is the same for every part. Nothing has to cross between parts.
Inputs may be any that keep to these rules, and one draw needn't show every extreme that they name: `dilations`: each dilation is a power of two; some layer has dilation 8.
All inputs are finite; a program needn't handle non-finite values.
Results may differ from the reference program's by a relative error of at most 0.0061.
Values may be sent and summed in bfloat16 or wider, within the bound.
No kernel may reach another device: no remote copies, remote signals or barrier semaphores. Data moves between devices by JAX's collectives and lax.ppermute only.
A program may use at most 64 MiB of HBM per device.

```python
import math
import jax
import jax.numpy as jnp
from jax import lax

C = 64
LAYERS = 6
DMAX = 8
P_SIZE = 256


def draw_dilations(key, part):
    levels = int(math.log2(DMAX)) + 1
    exponent = jax.random.randint(jax.random.fold_in(key, 11), (LAYERS,), 0, levels)
    chosen = jax.random.randint(jax.random.fold_in(key, 12), (), 0, LAYERS)
    exponent = jnp.where(jnp.arange(LAYERS) == chosen, levels - 1, exponent)
    return jnp.left_shift(jnp.ones((LAYERS,), jnp.int32), exponent.astype(jnp.int32)).astype(jnp.int32)


def level_of(stream_key, extent, shards, low, top_value):
    loudness, own = 1.0, jax.random.fold_in(stream_key, 6)
    for axis_at, blocks in shards:
        heights = jnp.exp(jax.random.uniform(jax.random.fold_in(own, axis_at), (blocks,), jnp.float32, low / len(shards), top_value / len(shards)))
        loudness = loudness * jnp.repeat(heights, extent[axis_at] // blocks).reshape([-1 if axis == axis_at else 1 for axis in range(len(extent))])
    return loudness


def bell_draw(own_key, dims, scale, limit, split=(), held_as=jnp.bfloat16):
    values = jax.random.normal(own_key, dims, jnp.float32) * scale
    if len(split) > 0:
        values = level_of(own_key, dims, split, -0.22, 0.18) * values
    return jnp.clip(values, min=-limit, max=limit).astype(held_as)


def setup_inputs(seed: int = 0, part: int = 0) -> dict:
    key_of = jax.random.split(jax.random.key(seed), 5)
    own_keys = jax.random.split(jax.random.fold_in(key_of[4], part), 5)
    return {
        "maps": bell_draw(own_keys[0], (C, P_SIZE, P_SIZE), 1.0, 6.0, ((1, 8), (2, 2))),
        "weights": bell_draw(key_of[1], (LAYERS, 3, 3, C, C), (9 * C) ** -0.5, 0.25),
        "biases": bell_draw(key_of[2], (LAYERS, C), 0.5, 3.0),
        "dilations": draw_dilations(jax.random.fold_in(key_of[4], 71), part),
    }


def conv_gelu(current, tap_weights, tap_bias, spacing):
    chans, height, width = current.shape
    padded = jnp.pad(current, ((0, 0), (DMAX, DMAX), (DMAX, DMAX)))
    summed = jnp.zeros((tap_weights.shape[2], height * width), jnp.float32)
    for tap_row in range(3):
        for tap_col in range(3):
            row_start = (DMAX + (tap_row - 1) * spacing).astype(jnp.int32)
            col_start = (DMAX + (tap_col - 1) * spacing).astype(jnp.int32)
            window = lax.dynamic_slice(padded, (jnp.int32(0), row_start, col_start), (chans, height, width))
            summed = summed + jnp.dot(tap_weights[tap_row, tap_col], window.reshape(chans, height * width), preferred_element_type=jnp.float32)
    branch = jax.nn.gelu(summed + tap_bias[:, None].astype(jnp.float32), approximate=False)
    return (current.astype(jnp.float32) + branch.reshape(current.shape)).astype(jnp.bfloat16)


def reference(maps, weights, biases, dilations):
    current = maps
    for layer in range(LAYERS):
        current = conv_gelu(current, weights[layer], biases[layer], dilations[layer])
        if layer == LAYERS // 2 - 1:
            flipped = jnp.swapaxes(current, 1, 2)
            current = (0.5 * (current.astype(jnp.float32) + flipped.astype(jnp.float32))).astype(jnp.bfloat16)
    return current
```

```python
import functools

import jax
import jax.numpy as jnp
from jax import lax
from jax.experimental import pallas as pl
from jax.experimental.pallas import tpu as pltpu
from jax.sharding import PartitionSpec as P

LAYERS = 6
DMAX = 8


def extended(block, sides, width):
    for axis, dim in sides:
        count = lax.axis_size(axis)
        forward = [(i, i + 1) for i in range(count - 1)]
        backward = [(target, source) for source, target in forward]
        low = lax.ppermute(
            lax.slice_in_dim(block, block.shape[dim] - width, None, axis=dim), axis, forward
        )
        high = lax.ppermute(lax.slice_in_dim(block, 0, width, axis=dim), axis, backward)
        block = jnp.concatenate([low, block, high], axis=dim)
    return block


def contribution(piece, weight_piece, spacing, row_count, col_count):
    count = piece.shape[0]
    out_count = weight_piece.shape[2]
    matrix = jnp.transpose(weight_piece, (2, 0, 1, 3)).reshape(out_count, 9 * count)
    block = 128
    results = []
    for block_index in range(col_count // block):
        windows = []
        for tap_row in range(3):
            for tap_col in range(3):
                row_start = DMAX + (tap_row - 1) * spacing
                col_start = DMAX + (tap_col - 1) * spacing + block_index * block
                windows.append(
                    lax.dynamic_slice(
                        piece, (jnp.int32(0), row_start, col_start), (count, row_count, block)
                    )
                )
        stacked = jnp.stack(windows, 0).reshape(9 * count, row_count * block)
        product = jnp.dot(matrix, stacked, preferred_element_type=jnp.float32)
        results.append(product.reshape(out_count, row_count, block))
    return jnp.concatenate(results, axis=2)


def finish(current, summed, tap_bias):
    branch = jax.nn.gelu(summed + tap_bias[:, None, None].astype(jnp.float32), approximate=False)
    return (current.astype(jnp.float32) + branch).astype(jnp.bfloat16)


def conv_whole(current, padded, tap_weights, tap_bias, spacing):
    summed = contribution(padded, tap_weights, spacing, current.shape[1], current.shape[2])
    return finish(current, summed, tap_bias)


def to_slab(current):
    return lax.all_to_all(current, "col", split_axis=1, concat_axis=2, tiled=True)


def to_tile(current):
    return lax.all_to_all(current, "col", split_axis=2, concat_axis=1, tiled=True)


def split_rows(current):
    return lax.all_to_all(current, "ch", split_axis=1, concat_axis=0, tiled=True)


def join_rows(current):
    return lax.all_to_all(current, "ch", split_axis=0, concat_axis=1, tiled=True)


def mirror(slab):
    flipped = jnp.swapaxes(slab, 1, 2)
    other = lax.all_to_all(flipped, ("row", "col"), split_axis=1, concat_axis=2, tiled=True)
    return (0.5 * (slab.astype(jnp.float32) + other.astype(jnp.float32))).astype(jnp.bfloat16)


def on_device(maps, weights, biases, dilations):
    layers_n = weights.shape[0]
    bias_block = biases.reshape(layers_n, 1, 1, biases.shape[1], 1)
    full_weights, full_bias = (
        lax.all_gather(weights, "ch", axis=3, tiled=True),
        lax.all_gather(bias_block, "ch", axis=3, tiled=True),
    )
    full_bias = full_bias.reshape(layers_n, full_bias.shape[3])
    current = split_rows(maps)
    for layer in range(LAYERS):
        padded = extended(current, ((("row", "ch"), 1), ("col", 2)), DMAX)
        current = conv_whole(
            current, padded, full_weights[layer], full_bias[layer], dilations[layer]
        )
        if layer == LAYERS // 2 - 1:
            current = split_rows(to_tile(mirror(to_slab(join_rows(current)))))
    return join_rows(current)


CH = 64
ROWS = 32
COLS = 128
HALF = LAYERS // 2
HALO = HALF * DMAX
SLOT = 32
FULL = ROWS + 2 * HALO
KDIM = 3 * CH + 16
UNROLL = 16
BF16 = jnp.bfloat16
F32 = jnp.float32


def place():
    r, c = lax.axis_index("row"), lax.axis_index("col")
    return r, c, lax.rem(r, 2)


def edge_pack(row_of, out_ref, c, start, groups):
    lane = lax.broadcasted_iota(jnp.int32, (CH, COLS), 1)
    for t in range(groups):
        acc = None
        for q in range(4):
            piece = pltpu.roll(row_of(start + t + groups * q), lax.rem(SLOT * (q + 1 - c), COLS), 1)
            acc = piece if acc is None else jnp.where(lane >= SLOT * q, piece, acc)
        out_ref[t] = acc.astype(BF16)


def pack_sends(read, a_ref, b_ref, c_ref, d_ref, e_ref, c, core):
    off_a = (ROWS - HALO) * (1 - core)
    off_b = (ROWS - HALO) * core
    for i in range(HALO):
        a_ref[i] = read(off_a + i)
        b_ref[i] = read(off_b + i)

    def row_of(i):
        return read(i).astype(F32)

    edge_pack(row_of, c_ref, c, 0, ROWS // 4)
    edge_pack(row_of, d_ref, c, off_a, HALO // 4)
    edge_pack(row_of, e_ref, c, off_b, HALO // 4)


def pack_kernel(x_ref, xt_ref, a_ref, b_ref, c_ref, d_ref, e_ref, flat):
    _, c, core = place()
    flat[...] = x_ref[...].reshape(CH * ROWS, COLS).astype(F32)
    for h in range(ROWS):
        xt_ref[h] = flat[pl.ds(h, CH, stride=ROWS), :].astype(BF16)
    pack_sends(lambda i: xt_ref[i], a_ref, b_ref, c_ref, d_ref, e_ref, c, core)


def assemble(xa, xt_ref, a_ref, b_ref, c_ref, d_ref, e_ref, c, core):
    lane = lax.broadcasted_iota(jnp.int32, (CH, COLS), 1)
    first = c * (COLS - SLOT)
    mask = (lane >= first) & (lane < first + SLOT)
    at_a = (FULL - HALO) * (1 - core)
    at_b = (FULL - HALO) * core
    for i in range(ROWS):
        xa[HALO + i, :, 0:COLS] = xt_ref[i]
    for i in range(HALO):
        xa[at_a + i, :, 0:COLS] = a_ref[i]
        xa[at_b + i, :, 0:COLS] = b_ref[i]
    for ref, start, groups in ((c_ref, HALO, ROWS // 4), (d_ref, at_a, HALO // 4), (e_ref, at_b, HALO // 4)):
        for t in range(groups):
            packed = ref[t].astype(F32)
            for q in range(4):
                piece = pltpu.roll(packed, lax.rem(COLS + first - SLOT * q, COLS), 1)
                xa[start + t + groups * q, :, COLS:] = jnp.where(mask, piece, 0.0).astype(BF16)
    return mask


def run_layers(base, dil_ref, w_ref, xa, xb, mask, last, row_count):
    r, _, _ = place()
    lo_map = jnp.where(r == 0, HALO, 0)
    hi_map = jnp.where(r == row_count - 1, HALO + ROWS, FULL)
    lane = lax.broadcasted_iota(jnp.int32, (CH, COLS), 1)
    ones = jnp.where(lax.broadcasted_iota(jnp.int32, (16, 2 * COLS), 0) == 0, 1.0, 0.0).astype(BF16)
    zeros = jnp.zeros((CH, 2 * COLS), BF16)
    for i in range(HALO):
        xb[i] = zeros
        xb[FULL - HALO + i] = zeros
    src, dst = xa, xb
    for layer in range(HALF):
        s = dil_ref[base + layer]
        rest = 0
        for later in range(layer + 1, HALF):
            rest = rest + dil_ref[base + later]
        final = layer == HALF - 1
        lo = jnp.maximum(HALO - rest, lo_map) if not final else jnp.int32(HALO)
        hi = jnp.minimum(HALO + ROWS + rest, hi_map) if not final else jnp.int32(HALO + ROWS)
        from_left, from_right = lane >= s, lane < COLS - s

        def row(h, src=src, dst=dst, s=s, layer=layer, fl=from_left, fr=from_right, final=final):
            taps = jnp.concatenate([src[h - s], src[h], src[h + s], ones], axis=0)
            y = jnp.dot(w_ref[layer], taps, preferred_element_type=F32)
            left = [pltpu.roll(y[0:CH, k * COLS : (k + 1) * COLS], s, 1) for k in range(2)]
            right = [pltpu.roll(y[2 * CH :, k * COLS : (k + 1) * COLS], COLS - s, 1) for k in range(2)]
            for k in range(1 if final else 2):
                half = (
                    y[CH : 2 * CH, k * COLS : (k + 1) * COLS]
                    + jnp.where(fl, left[k], left[1 - k])
                    + jnp.where(fr, right[k], right[1 - k])
                )
                branch = half + half * lax.erf(half * 1.4142135623730951)
                new = src[h, :, k * COLS : (k + 1) * COLS].astype(F32) + branch
                if final:
                    last(h - HALO, new)
                elif k == 0:
                    dst[h, :, 0:COLS] = new.astype(BF16)
                else:
                    dst[h, :, COLS:] = jnp.where(mask, new, 0.0).astype(BF16)

        def step(i, _, lo=lo, hi=hi, row=row):
            first = jnp.minimum(lo + i * UNROLL, hi - UNROLL)
            for u in range(UNROLL):
                row(first + u)
            return 0

        lax.fori_loop(0, (hi - lo + UNROLL - 1) // UNROLL, step, 0)
        src, dst = dst, src


def first_kernel(row_count, dil_ref, w_ref, xt_ref, a_ref, b_ref, c_ref, d_ref, e_ref,
                 x_ref, m0, m1, m2, m3, xa, xb, flat, turned):
    r, c, core = place()
    mask = assemble(xa, xt_ref, a_ref, b_ref, c_ref, d_ref, e_ref, c, core)

    def last(h, new):
        rounded = new.astype(BF16)
        x_ref[h] = rounded
        flat[pl.ds(h, CH, stride=ROWS), :] = rounded.astype(F32)

    run_layers(0, dil_ref, w_ref, xa, xb, mask, last, row_count)
    for g in range(16):
        four = jnp.concatenate([flat[(16 * k + g) * ROWS : (16 * k + g + 1) * ROWS, :] for k in range(4)], axis=0)
        turned[pl.ds(g, COLS, stride=16), :] = four.T
    rr = lax.rem(r, 4)
    for k, ref in enumerate((m0, m1, m2, m3)):
        start = pl.multiple_of(jnp.bitwise_xor(rr, k) * (ROWS * 16), ROWS * 16)
        ref[...] = turned[pl.ds(start, ROWS * 16), :].reshape(ROWS, 16, COLS).astype(BF16)


def mirror_kernel(x_ref, m0, m1, m2, m3, xt_ref, a_ref, b_ref, c_ref, d_ref, e_ref, got):
    r, c, core = place()
    rr = lax.rem(r, 4)
    for k, ref in enumerate((m0, m1, m2, m3)):
        got[jnp.bitwise_xor(rr, k)] = ref[...]
    slot = lax.broadcasted_iota(jnp.int32, (16, COLS), 1) // SLOT

    def by_slot(pieces):
        out = pieces[0]
        for q in range(1, 4):
            out = jnp.where(slot >= q, pieces[q], out)
        return out

    for i in range(ROWS):
        parts = [got[q, i].astype(F32) for q in range(4)]
        moved = []
        for d in range(4):
            v = by_slot([parts[(q + d) % 4] for q in range(4)])
            moved.append(pltpu.roll(v, SLOT * d, 1) if d else v)
        mirrored = jnp.concatenate(
            [by_slot([moved[(q - k) % 4] for q in range(4)]) for k in range(4)], axis=0
        )
        xt_ref[i] = (0.5 * (x_ref[i].astype(F32) + mirrored)).astype(BF16)
    pack_sends(lambda i: xt_ref[i], a_ref, b_ref, c_ref, d_ref, e_ref, c, core)


def second_kernel(row_count, dil_ref, w_ref, xt_ref, a_ref, b_ref, c_ref, d_ref, e_ref, o_ref, xa, xb, flat):
    _, c, core = place()
    mask = assemble(xa, xt_ref, a_ref, b_ref, c_ref, d_ref, e_ref, c, core)

    def last(h, new):
        flat[pl.ds(h, CH, stride=ROWS), :] = new

    run_layers(HALF, dil_ref, w_ref, xa, xb, mask, last, row_count)
    o_ref[...] = flat[...].reshape(CH, ROWS, COLS).astype(BF16)


def kernel_call(body, outs, scratch, operands, smem=0, cost=None):
    vmem = pl.BlockSpec(memory_space=pltpu.VMEM)
    return pl.pallas_call(
        body,
        out_shape=[jax.ShapeDtypeStruct(shape, BF16) for shape in outs],
        in_specs=[pl.BlockSpec(memory_space=pltpu.SMEM)] * smem + [vmem] * (len(operands) - smem),
        out_specs=[vmem] * len(outs),
        scratch_shapes=[pltpu.VMEM(shape, dtype) for shape, dtype in scratch],
        compiler_params=pltpu.CompilerParams(vmem_limit_bytes=48 << 20),
        cost_estimate=cost,
    )(*operands)


SENDS = [(HALO, CH, COLS), (HALO, CH, COLS), (ROWS // 4, CH, COLS), (HALO // 4, CH, COLS), (HALO // 4, CH, COLS)]
TILE = (ROWS, CH, COLS)


def swap_halos(sends, row_count):
    both = [(r, c) for r in range(row_count) for c in range(2)]

    def swap(x, partner):
        perm = [(2 * r + c, 2 * partner(r, c)[0] + partner(r, c)[1]) for r, c in both if 0 <= partner(r, c)[0] < row_count]
        return lax.ppermute(x, ("row", "col"), perm)

    a, b, c, d, e = sends
    across = lambda r: r - 1 if r % 2 == 0 else r + 1
    got_e = swap(e, lambda r, c: (across(r), 1 - c))
    got_b = swap(b, lambda r, c: (across(r), c))
    got_c = swap(c, lambda r, c: (r, 1 - c))
    got_d = swap(d, lambda r, c: (r ^ 1, 1 - c))
    got_a = swap(a, lambda r, c: (r ^ 1, c))
    return got_a, got_b, got_c, got_d, got_e


def swap_mirror(blocks, row_count):
    out = []
    for k, x in enumerate(blocks):
        perm = [(2 * r + c, 2 * (4 * c + ((r % 4) ^ k)) + r // 4) for r in range(row_count) for c in range(2)]
        out.append(lax.ppermute(x, ("row", "col"), perm))
    return out


def on_tile(row_count, maps, weights, biases, dilations):
    half = weights.transpose(0, 2, 3, 1, 4).reshape(LAYERS, 3 * CH, 3 * CH) * jnp.asarray(0.5, BF16)
    bias = jnp.pad((biases * jnp.asarray(0.5, BF16))[:, :, None], ((0, 0), (CH, CH), (0, KDIM - 3 * CH - 1)))
    matrices = jnp.concatenate([half, bias], axis=2)

    tile, *sends = kernel_call(pack_kernel, [TILE] + SENDS, [((CH * ROWS, COLS), F32)], [maps])
    halos = swap_halos(sends, row_count)
    work = [((FULL, CH, 2 * COLS), BF16)] * 2 + [((CH * ROWS, COLS), F32)]
    tile, *blocks = kernel_call(
        functools.partial(first_kernel, row_count),
        [TILE] + [(ROWS, 16, COLS)] * 4,
        work + [((COLS * 16, COLS), F32)],
        [dilations, matrices[:HALF], tile, *halos],
        smem=1,
    )
    blocks = swap_mirror(blocks, row_count)
    tile, *sends = kernel_call(
        mirror_kernel, [TILE] + SENDS, [((4, ROWS, 16, COLS), BF16)], [tile, *blocks]
    )
    halos = swap_halos(sends, row_count)
    (out,) = kernel_call(
        functools.partial(second_kernel, row_count),
        [(CH, ROWS, COLS)],
        work,
        [dilations, matrices[HALF:], tile, *halos],
        smem=1,
    )
    return out


def solution(mesh):
    def step(maps, weights, biases, dilations):
        sizes = mesh.shape
        tiled = (
            sizes["ch"] == 1
            and sizes["col"] == 2
            and sizes["row"] == 8
            and maps.shape == (CH, ROWS * sizes["row"] * sizes["grp"], COLS * 2)
        )
        body = functools.partial(on_tile, sizes["row"]) if tiled else on_device
        return jax.shard_map(
            body,
            mesh=mesh,
            in_specs=(
                P("ch", ("grp", "row"), "col"),
                P(None, None, None, "ch", None),
                P(None, "ch"),
                P(),
            ),
            out_specs=P("ch", ("grp", "row"), "col"),
            check_vma=False,
        )(maps, weights, biases, dilations)

    return step
```

```python
import functools

import jax
import jax.numpy as jnp
from jax import lax
from jax.experimental import pallas as pl
from jax.experimental.pallas import tpu as pltpu
from jax.sharding import PartitionSpec as P

LAYERS = 6
DMAX = 8


def extended(block, sides, width):
    for axis, dim in sides:
        count = lax.axis_size(axis)
        forward = [(i, i + 1) for i in range(count - 1)]
        backward = [(target, source) for source, target in forward]
        low = lax.ppermute(
            lax.slice_in_dim(block, block.shape[dim] - width, None, axis=dim), axis, forward
        )
        high = lax.ppermute(lax.slice_in_dim(block, 0, width, axis=dim), axis, backward)
        block = jnp.concatenate([low, block, high], axis=dim)
    return block


def contribution(piece, weight_piece, spacing, row_count, col_count):
    count = piece.shape[0]
    out_count = weight_piece.shape[2]
    matrix = jnp.transpose(weight_piece, (2, 0, 1, 3)).reshape(out_count, 9 * count)
    block = 128
    results = []
    for block_index in range(col_count // block):
        windows = []
        for tap_row in range(3):
            for tap_col in range(3):
                row_start = DMAX + (tap_row - 1) * spacing
                col_start = DMAX + (tap_col - 1) * spacing + block_index * block
                windows.append(
                    lax.dynamic_slice(
                        piece, (jnp.int32(0), row_start, col_start), (count, row_count, block)
                    )
                )
        stacked = jnp.stack(windows, 0).reshape(9 * count, row_count * block)
        product = jnp.dot(matrix, stacked, preferred_element_type=jnp.float32)
        results.append(product.reshape(out_count, row_count, block))
    return jnp.concatenate(results, axis=2)


def finish(current, summed, tap_bias):
    branch = jax.nn.gelu(summed + tap_bias[:, None, None].astype(jnp.float32), approximate=False)
    return (current.astype(jnp.float32) + branch).astype(jnp.bfloat16)


def conv_whole(current, padded, tap_weights, tap_bias, spacing):
    summed = contribution(padded, tap_weights, spacing, current.shape[1], current.shape[2])
    return finish(current, summed, tap_bias)


def to_slab(current):
    return lax.all_to_all(current, "col", split_axis=1, concat_axis=2, tiled=True)


def to_tile(current):
    return lax.all_to_all(current, "col", split_axis=2, concat_axis=1, tiled=True)


def split_rows(current):
    return lax.all_to_all(current, "ch", split_axis=1, concat_axis=0, tiled=True)


def join_rows(current):
    return lax.all_to_all(current, "ch", split_axis=0, concat_axis=1, tiled=True)


def mirror(slab):
    flipped = jnp.swapaxes(slab, 1, 2)
    other = lax.all_to_all(flipped, ("row", "col"), split_axis=1, concat_axis=2, tiled=True)
    return (0.5 * (slab.astype(jnp.float32) + other.astype(jnp.float32))).astype(jnp.bfloat16)


def on_device(maps, weights, biases, dilations):
    layers_n = weights.shape[0]
    bias_block = biases.reshape(layers_n, 1, 1, biases.shape[1], 1)
    full_weights, full_bias = (
        lax.all_gather(weights, "ch", axis=3, tiled=True),
        lax.all_gather(bias_block, "ch", axis=3, tiled=True),
    )
    full_bias = full_bias.reshape(layers_n, full_bias.shape[3])
    current = split_rows(maps)
    for layer in range(LAYERS):
        padded = extended(current, ((("row", "ch"), 1), ("col", 2)), DMAX)
        current = conv_whole(
            current, padded, full_weights[layer], full_bias[layer], dilations[layer]
        )
        if layer == LAYERS // 2 - 1:
            current = split_rows(to_tile(mirror(to_slab(join_rows(current)))))
    return join_rows(current)


CH = 64
ROWS = 32
COLS = 128
HALF = LAYERS // 2
HALO = HALF * DMAX
EDGE_SLOTS = COLS // HALO
SLOT = 32
FULL = ROWS + 2 * HALO
KDIM = 3 * CH + 16
UNROLL = 16
BF16 = jnp.bfloat16
F32 = jnp.float32


def place():
    r, c = lax.axis_index("row"), lax.axis_index("col")
    return r, c, lax.rem(r, 2)


def edge_groups(rows):
    return -(-rows // EDGE_SLOTS)


def edge_pack(row_of, out_ref, c, start, rows):
    lane = lax.broadcasted_iota(jnp.int32, (CH, COLS), 1)
    groups = edge_groups(rows)
    for t in range(groups):
        acc = None
        for q in range(EDGE_SLOTS):
            i = t + groups * q
            if i < rows:
                piece = pltpu.roll(row_of(start + i), lax.rem(HALO * (q + 1 - c) + c * COLS, COLS), 1)
                acc = piece if acc is None else jnp.where(lane >= HALO * q, piece, acc)
        out_ref[t] = acc.astype(BF16)


def pack_sends(read, a_ref, b_ref, c_ref, d_ref, e_ref, c, core):
    off_a = (ROWS - HALO) * (1 - core)
    off_b = (ROWS - HALO) * core
    for i in range(HALO):
        a_ref[i] = read(off_a + i)
        b_ref[i] = read(off_b + i)

    def row_of(i):
        return read(i).astype(F32)

    edge_pack(row_of, c_ref, c, 0, ROWS)
    edge_pack(row_of, d_ref, c, off_a, HALO)
    edge_pack(row_of, e_ref, c, off_b, HALO)


def pack_kernel(x_ref, xt_ref, a_ref, b_ref, c_ref, d_ref, e_ref, flat):
    _, c, core = place()
    flat[...] = x_ref[...].reshape(CH * ROWS, COLS).astype(F32)
    for h in range(ROWS):
        xt_ref[h] = flat[pl.ds(h, CH, stride=ROWS), :].astype(BF16)
    pack_sends(lambda i: xt_ref[i], a_ref, b_ref, c_ref, d_ref, e_ref, c, core)


def assemble(xa, xt_ref, a_ref, b_ref, c_ref, d_ref, e_ref, c, core):
    lane = lax.broadcasted_iota(jnp.int32, (CH, COLS), 1)
    first = c * (COLS - HALO)
    mask = (lane >= first) & (lane < first + HALO)
    at_a = (FULL - HALO) * (1 - core)
    at_b = (FULL - HALO) * core
    for i in range(ROWS):
        xa[HALO + i, :, 0:COLS] = xt_ref[i]
    for i in range(HALO):
        xa[at_a + i, :, 0:COLS] = a_ref[i]
        xa[at_b + i, :, 0:COLS] = b_ref[i]
    for ref, start, rows in ((c_ref, HALO, ROWS), (d_ref, at_a, HALO), (e_ref, at_b, HALO)):
        groups = edge_groups(rows)
        for t in range(groups):
            packed = ref[t].astype(F32)
            for q in range(EDGE_SLOTS):
                i = t + groups * q
                if i < rows:
                    piece = pltpu.roll(packed, lax.rem(COLS + first - HALO * q, COLS), 1)
                    xa[start + i, :, COLS:] = jnp.where(mask, piece, 0.0).astype(BF16)
    return mask


def run_layers(base, dil_ref, w_ref, xa, xb, mask, last, row_count):
    r, _, _ = place()
    lo_map = jnp.where(r == 0, HALO, 0)
    hi_map = jnp.where(r == row_count - 1, HALO + ROWS, FULL)
    lane = lax.broadcasted_iota(jnp.int32, (CH, COLS), 1)
    ones = jnp.where(lax.broadcasted_iota(jnp.int32, (16, 2 * COLS), 0) == 0, 1.0, 0.0).astype(BF16)
    zeros = jnp.zeros((CH, 2 * COLS), BF16)
    for i in range(HALO):
        xb[i] = zeros
        xb[FULL - HALO + i] = zeros
    src, dst = xa, xb
    for layer in range(HALF):
        s = dil_ref[base + layer]
        rest = 0
        for later in range(layer + 1, HALF):
            rest = rest + dil_ref[base + later]
        final = layer == HALF - 1
        lo = jnp.maximum(HALO - rest, lo_map) if not final else jnp.int32(HALO)
        hi = jnp.minimum(HALO + ROWS + rest, hi_map) if not final else jnp.int32(HALO + ROWS)
        from_left, from_right = lane >= s, lane < COLS - s

        def row(h, src=src, dst=dst, s=s, layer=layer, fl=from_left, fr=from_right, final=final):
            taps = jnp.concatenate([src[h - s], src[h], src[h + s], ones], axis=0)
            y = jnp.dot(w_ref[base + layer], taps, preferred_element_type=F32)
            left = [pltpu.roll(y[0:CH, k * COLS : (k + 1) * COLS], s, 1) for k in range(2)]
            right = [pltpu.roll(y[2 * CH :, k * COLS : (k + 1) * COLS], COLS - s, 1) for k in range(2)]
            for k in range(1 if final else 2):
                half = (
                    y[CH : 2 * CH, k * COLS : (k + 1) * COLS]
                    + jnp.where(fl, left[k], left[1 - k])
                    + jnp.where(fr, right[k], right[1 - k])
                )
                branch = half + half * lax.erf(half * 1.4142135623730951)
                new = src[h, :, k * COLS : (k + 1) * COLS].astype(F32) + branch
                if final:
                    last(h - HALO, new)
                elif k == 0:
                    dst[h, :, 0:COLS] = new.astype(BF16)
                else:
                    dst[h, :, COLS:] = jnp.where(mask, new, 0.0).astype(BF16)

        def step(i, _, lo=lo, hi=hi, row=row):
            first = jnp.minimum(lo + i * UNROLL, hi - UNROLL)
            for u in range(UNROLL):
                row(first + u)
            return 0

        lax.fori_loop(0, (hi - lo + UNROLL - 1) // UNROLL, step, 0)
        src, dst = dst, src


def weights_kernel(w_ref, bias_ref, o_ref):
    row = lax.broadcasted_iota(jnp.int32, (CH, CH), 0)
    col = lax.broadcasted_iota(jnp.int32, (CH, CH), 1)
    lane = lax.broadcasted_iota(jnp.int32, (CH, KDIM - 3 * CH), 1)
    for layer in range(LAYERS):
        bias = jnp.broadcast_to(bias_ref[layer : layer + 1, :].astype(F32) * 0.5, (CH, CH))
        column = jnp.sum(jnp.where(row == col, bias, 0.0), axis=1, keepdims=True)
        extra = jnp.where(lane == 0, column, 0.0).astype(BF16)
        none = jnp.zeros((CH, KDIM - 3 * CH), BF16)
        for b in range(3):
            taps = jnp.concatenate([w_ref[layer, a, b] for a in range(3)], axis=1)
            o_ref[layer, b * CH : (b + 1) * CH, 0 : 3 * CH] = (taps.astype(F32) * 0.5).astype(BF16)
            o_ref[layer, b * CH : (b + 1) * CH, 3 * CH :] = extra if b == 1 else none


def first_kernel(row_count, dil_ref, w_ref, xt_ref, a_ref, b_ref, c_ref, d_ref, e_ref,
                 x_ref, m0, m1, m2, m3, xa, xb, flat, turned):
    r, c, core = place()
    mask = assemble(xa, xt_ref, a_ref, b_ref, c_ref, d_ref, e_ref, c, core)

    def last(h, new):
        rounded = new.astype(BF16)
        x_ref[h] = rounded
        flat[pl.ds(h, CH, stride=ROWS), :] = rounded.astype(F32)

    run_layers(0, dil_ref, w_ref, xa, xb, mask, last, row_count)
    for g in range(16):
        four = jnp.concatenate([flat[(16 * k + g) * ROWS : (16 * k + g + 1) * ROWS, :] for k in range(4)], axis=0)
        turned[pl.ds(g, COLS, stride=16), :] = four.T
    rr = lax.rem(r, 4)
    for k, ref in enumerate((m0, m1, m2, m3)):
        start = pl.multiple_of(jnp.bitwise_xor(rr, k) * (ROWS * 16), ROWS * 16)
        ref[...] = turned[pl.ds(start, ROWS * 16), :].reshape(ROWS, 16, COLS).astype(BF16)


def mirror_kernel(x_ref, own, m0, m1, m2, m3, xt_ref, a_ref, b_ref, c_ref, d_ref, e_ref, got):
    r, c, core = place()
    rr = lax.rem(r, 4)
    for k, ref in enumerate((m0, m1, m2, m3)):
        got[jnp.bitwise_xor(rr, k)] = ref[...]

    @pl.when(r // 4 == c)
    def _():
        got[rr] = own[...]

    slot = lax.broadcasted_iota(jnp.int32, (16, COLS), 1) // SLOT

    def by_slot(pieces):
        out = pieces[0]
        for q in range(1, 4):
            out = jnp.where(slot >= q, pieces[q], out)
        return out

    for i in range(ROWS):
        parts = [got[q, i].astype(F32) for q in range(4)]
        moved = []
        for d in range(4):
            v = by_slot([parts[(q + d) % 4] for q in range(4)])
            moved.append(pltpu.roll(v, SLOT * d, 1) if d else v)
        mirrored = jnp.concatenate(
            [by_slot([moved[(q - k) % 4] for q in range(4)]) for k in range(4)], axis=0
        )
        xt_ref[i] = (0.5 * (x_ref[i].astype(F32) + mirrored)).astype(BF16)
    pack_sends(lambda i: xt_ref[i], a_ref, b_ref, c_ref, d_ref, e_ref, c, core)


def second_kernel(row_count, dil_ref, w_ref, xt_ref, a_ref, b_ref, c_ref, d_ref, e_ref, o_ref, xa, xb, flat):
    _, c, core = place()
    mask = assemble(xa, xt_ref, a_ref, b_ref, c_ref, d_ref, e_ref, c, core)

    def last(h, new):
        flat[pl.ds(h, CH, stride=ROWS), :] = new

    run_layers(HALF, dil_ref, w_ref, xa, xb, mask, last, row_count)
    o_ref[...] = flat[...].reshape(CH, ROWS, COLS).astype(BF16)


def kernel_call(body, outs, scratch, operands, smem=0, cost=None):
    vmem = pl.BlockSpec(memory_space=pltpu.VMEM)
    return pl.pallas_call(
        body,
        out_shape=[jax.ShapeDtypeStruct(shape, BF16) for shape in outs],
        in_specs=[pl.BlockSpec(memory_space=pltpu.SMEM)] * smem + [vmem] * (len(operands) - smem),
        out_specs=[vmem] * len(outs),
        scratch_shapes=[pltpu.VMEM(shape, dtype) for shape, dtype in scratch],
        compiler_params=pltpu.CompilerParams(vmem_limit_bytes=48 << 20),
        cost_estimate=cost,
    )(*operands)


ROW_SENDS = [(HALO, CH, COLS)] * 2
EDGE_SENDS = [(edge_groups(rows), CH, COLS) for rows in (ROWS, HALO, HALO)]
SENDS = ROW_SENDS + EDGE_SENDS
TILE = (ROWS, CH, COLS)


def swap_halos(sends, row_count):
    both = [(r, c) for r in range(row_count) for c in range(2)]

    def swap(x, partner):
        perm = [(2 * r + c, 2 * partner(r, c)[0] + partner(r, c)[1]) for r, c in both if 0 <= partner(r, c)[0] < row_count]
        return lax.ppermute(x, ("row", "col"), perm)

    a, b, c, d, e = sends
    across = lambda r: r - 1 if r % 2 == 0 else r + 1
    got_e = swap(e, lambda r, c: (across(r), 1 - c))
    got_b = swap(b, lambda r, c: (across(r), c))
    got_c = swap(c, lambda r, c: (r, 1 - c))
    got_d = swap(d, lambda r, c: (r ^ 1, 1 - c))
    got_a = swap(a, lambda r, c: (r ^ 1, c))
    return got_a, got_b, got_c, got_d, got_e


def swap_mirror(blocks, row_count):
    both = [(r, c) for r in range(row_count) for c in range(2)]
    near = [(r, c) for r, c in both if r // 4 == c]
    far = [(r, c) for r, c in both if r // 4 != c]

    def send(x, sources, target):
        return lax.ppermute(x, ("row", "col"), [(2 * r + c, 2 * target(r, c)[0] + target(r, c)[1]) for r, c in sources])

    crossed = send(blocks[0], far, lambda r, c: (r, 1 - c))
    out = [send(blocks[k], both, lambda r, c, k=k: (4 * c + ((r % 4) ^ k), r // 4)) for k in range(1, 4)]
    return [send(crossed, near, lambda r, c: (r ^ 4, c)), *out]


def on_tile(row_count, maps, weights, biases, dilations):
    (matrices,) = kernel_call(weights_kernel, [(LAYERS, 3 * CH, KDIM)], [], [weights, biases])
    tile, *sends = kernel_call(pack_kernel, [TILE] + SENDS, [((CH * ROWS, COLS), F32)], [maps])
    halos = swap_halos(sends, row_count)
    work = [((FULL, CH, 2 * COLS), BF16)] * 2 + [((CH * ROWS, COLS), F32)]
    tile, *blocks = kernel_call(
        functools.partial(first_kernel, row_count),
        [TILE] + [(ROWS, 16, COLS)] * 4,
        work + [((COLS * 16, COLS), F32)],
        [dilations, matrices, tile, *halos],
        smem=1,
    )
    mirrored = swap_mirror(blocks, row_count)
    tile, *sends = kernel_call(
        mirror_kernel, [TILE] + SENDS, [((4, ROWS, 16, COLS), BF16)], [tile, blocks[0], *mirrored]
    )
    halos = swap_halos(sends, row_count)
    (out,) = kernel_call(
        functools.partial(second_kernel, row_count),
        [(CH, ROWS, COLS)],
        work,
        [dilations, matrices, tile, *halos],
        smem=1,
    )
    return out


def solution(mesh):
    def step(maps, weights, biases, dilations):
        sizes = mesh.shape
        tiled = (
            sizes["ch"] == 1
            and sizes["col"] == 2
            and sizes["row"] == 8
            and maps.shape == (CH, ROWS * sizes["row"] * sizes["grp"], COLS * 2)
        )
        body = functools.partial(on_tile, sizes["row"]) if tiled else on_device
        return jax.shard_map(
            body,
            mesh=mesh,
            in_specs=(
                P("ch", ("grp", "row"), "col"),
                P(None, None, None, "ch", None),
                P(None, "ch"),
                P(),
            ),
            out_specs=P("ch", ("grp", "row"), "col"),
            check_vma=False,
        )(maps, weights, biases, dilations)

    return step
```

```python
import functools

import jax
import jax.numpy as jnp
from jax import lax
from jax.experimental import pallas as pl
from jax.experimental.pallas import tpu as pltpu
from jax.sharding import PartitionSpec as P

LAYERS = 6
DMAX = 8


def extended(block, sides, width):
    for axis, dim in sides:
        count = lax.axis_size(axis)
        forward = [(i, i + 1) for i in range(count - 1)]
        backward = [(target, source) for source, target in forward]
        low = lax.ppermute(
            lax.slice_in_dim(block, block.shape[dim] - width, None, axis=dim), axis, forward
        )
        high = lax.ppermute(lax.slice_in_dim(block, 0, width, axis=dim), axis, backward)
        block = jnp.concatenate([low, block, high], axis=dim)
    return block


def contribution(piece, weight_piece, spacing, row_count, col_count):
    count = piece.shape[0]
    out_count = weight_piece.shape[2]
    matrix = jnp.transpose(weight_piece, (2, 0, 1, 3)).reshape(out_count, 9 * count)
    block = 128
    results = []
    for block_index in range(col_count // block):
        windows = []
        for tap_row in range(3):
            for tap_col in range(3):
                row_start = DMAX + (tap_row - 1) * spacing
                col_start = DMAX + (tap_col - 1) * spacing + block_index * block
                windows.append(
                    lax.dynamic_slice(
                        piece, (jnp.int32(0), row_start, col_start), (count, row_count, block)
                    )
                )
        stacked = jnp.stack(windows, 0).reshape(9 * count, row_count * block)
        product = jnp.dot(matrix, stacked, preferred_element_type=jnp.float32)
        results.append(product.reshape(out_count, row_count, block))
    return jnp.concatenate(results, axis=2)


def finish(current, summed, tap_bias):
    branch = jax.nn.gelu(summed + tap_bias[:, None, None].astype(jnp.float32), approximate=False)
    return (current.astype(jnp.float32) + branch).astype(jnp.bfloat16)


def conv_whole(current, padded, tap_weights, tap_bias, spacing):
    summed = contribution(padded, tap_weights, spacing, current.shape[1], current.shape[2])
    return finish(current, summed, tap_bias)


def to_slab(current):
    return lax.all_to_all(current, "col", split_axis=1, concat_axis=2, tiled=True)


def to_tile(current):
    return lax.all_to_all(current, "col", split_axis=2, concat_axis=1, tiled=True)


def split_rows(current):
    return lax.all_to_all(current, "ch", split_axis=1, concat_axis=0, tiled=True)


def join_rows(current):
    return lax.all_to_all(current, "ch", split_axis=0, concat_axis=1, tiled=True)


def mirror(slab):
    flipped = jnp.swapaxes(slab, 1, 2)
    other = lax.all_to_all(flipped, ("row", "col"), split_axis=1, concat_axis=2, tiled=True)
    return (0.5 * (slab.astype(jnp.float32) + other.astype(jnp.float32))).astype(jnp.bfloat16)


def on_device(maps, weights, biases, dilations):
    layers_n = weights.shape[0]
    bias_block = biases.reshape(layers_n, 1, 1, biases.shape[1], 1)
    full_weights, full_bias = (
        lax.all_gather(weights, "ch", axis=3, tiled=True),
        lax.all_gather(bias_block, "ch", axis=3, tiled=True),
    )
    full_bias = full_bias.reshape(layers_n, full_bias.shape[3])
    current = split_rows(maps)
    for layer in range(LAYERS):
        padded = extended(current, ((("row", "ch"), 1), ("col", 2)), DMAX)
        current = conv_whole(
            current, padded, full_weights[layer], full_bias[layer], dilations[layer]
        )
        if layer == LAYERS // 2 - 1:
            current = split_rows(to_tile(mirror(to_slab(join_rows(current)))))
    return join_rows(current)


CH = 64
ROWS = 32
COLS = 128
HALF = LAYERS // 2
HALO = HALF * DMAX
EDGE_SLOTS = COLS // HALO
SLOT = 32
FULL = ROWS + 2 * HALO
KDIM = 3 * CH + 16
UNROLL = 24
BF16 = jnp.bfloat16
F32 = jnp.float32


def place():
    r, c = lax.axis_index("row"), lax.axis_index("col")
    return r, c, lax.rem(r, 2)


EDGE_GROUPS = -(-ROWS // EDGE_SLOTS)


def pack_sends(read, a_ref, b_ref, c_ref, c, core):
    off_a = (ROWS - HALO) * (1 - core)
    off_b = (ROWS - HALO) * core
    for i in range(HALO):
        a_ref[i] = read(off_a + i)
        b_ref[i] = read(off_b + i)
    lane = lax.broadcasted_iota(jnp.int32, (CH, COLS), 1)
    for t in range(EDGE_GROUPS):
        acc = None
        for q in range(EDGE_SLOTS):
            i = t + EDGE_GROUPS * q
            if i < ROWS:
                piece = pltpu.roll(read(i), lax.rem(HALO * (q + 1 - c) + c * COLS, COLS), 1)
                acc = piece if acc is None else jnp.where(lane >= HALO * q, piece, acc)
        c_ref[t] = acc


CHUNK = 16


def pack_kernel(x_ref, xt_ref, a_ref, b_ref, c_ref, raw, flat, sems):
    _, c, core = place()
    copies = []
    for k in range(CH // CHUNK):
        part = pl.ds(k * CHUNK, CHUNK)
        copies.append(pltpu.make_async_copy(x_ref.at[part], raw.at[part], sems.at[k]))
        copies[k].start()
    for k, copy in enumerate(copies):
        copy.wait()
        first = k * CHUNK
        flat[first * ROWS : (first + CHUNK) * ROWS, :] = raw[first : first + CHUNK].reshape(CHUNK * ROWS, COLS).astype(F32)
        for h in range(ROWS):
            xt_ref[h, first : first + CHUNK, :] = flat[pl.ds(first * ROWS + h, CHUNK, stride=ROWS), :].astype(BF16)
    pack_sends(lambda i: xt_ref[i], a_ref, b_ref, c_ref, c, core)


def assemble(xa, xt_ref, a_ref, b_ref, c_ref, d_ref, e_ref, c, core):
    lane = lax.broadcasted_iota(jnp.int32, (CH, COLS), 1)
    first = c * (COLS - HALO)
    mask = (lane >= first) & (lane < first + HALO)
    at_a = (FULL - HALO) * (1 - core)
    at_b = (FULL - HALO) * core
    for i in range(ROWS):
        xa[HALO + i, :, 0:COLS] = xt_ref[i]
    for i in range(HALO):
        xa[at_a + i, :, 0:COLS] = a_ref[i]
        xa[at_b + i, :, 0:COLS] = b_ref[i]
    nil = jnp.zeros((CH, COLS), BF16)
    other = ROWS - HALO
    for ref, start, skip, rows in ((c_ref, HALO, 0, ROWS), (d_ref, at_a, other * core, HALO), (e_ref, at_b, other * (1 - core), HALO)):
        for i in range(rows):
            t, q = lax.rem(i + skip, EDGE_GROUPS), lax.div(i + skip, EDGE_GROUPS)
            piece = pltpu.roll(ref[t], lax.rem(COLS + first - HALO * q, COLS), 1)
            xa[start + i, :, COLS:] = jnp.where(mask, piece, nil)
    return mask


def run_layers(base, dil_ref, w_ref, xa, xb, mask, last, row_count):
    r, _, _ = place()
    lo_map = jnp.where(r == 0, HALO, 0)
    hi_map = jnp.where(r == row_count - 1, HALO + ROWS, FULL)
    lane = lax.broadcasted_iota(jnp.int32, (CH, COLS), 1)
    ones = jnp.where(lax.broadcasted_iota(jnp.int32, (16, 2 * COLS), 0) == 0, 1.0, 0.0).astype(BF16)
    zeros = jnp.zeros((CH, 2 * COLS), BF16)
    for i in range(HALO):
        xb[i] = zeros
        xb[FULL - HALO + i] = zeros
    src, dst = xa, xb
    for layer in range(HALF):
        s = dil_ref[base + layer]
        rest = 0
        for later in range(layer + 1, HALF):
            rest = rest + dil_ref[base + later]
        final = layer == HALF - 1
        lo = jnp.maximum(HALO - rest, lo_map) if not final else jnp.int32(HALO)
        hi = jnp.minimum(HALO + ROWS + rest, hi_map) if not final else jnp.int32(HALO + ROWS)
        from_left, from_right = lane >= s, lane < COLS - s

        def row(h, src=src, dst=dst, s=s, layer=layer, fl=from_left, fr=from_right, final=final):
            taps = jnp.concatenate([src[h - s], src[h], src[h + s], ones], axis=0)
            y = jnp.dot(w_ref[base + layer], taps, preferred_element_type=F32)
            left = [pltpu.roll(y[0:CH, k * COLS : (k + 1) * COLS], s, 1) for k in range(2)]
            right = [pltpu.roll(y[2 * CH :, k * COLS : (k + 1) * COLS], COLS - s, 1) for k in range(2)]
            for k in range(1 if final else 2):
                half = (
                    y[CH : 2 * CH, k * COLS : (k + 1) * COLS]
                    + jnp.where(fl, left[k], left[1 - k])
                    + jnp.where(fr, right[k], right[1 - k])
                )
                branch = half + half * lax.erf(half * 1.4142135623730951)
                new = src[h, :, k * COLS : (k + 1) * COLS].astype(F32) + branch
                if final:
                    last(h - HALO, new)
                elif k == 0:
                    dst[h, :, 0:COLS] = new.astype(BF16)
                else:
                    dst[h, :, COLS:] = jnp.where(mask, new, 0.0).astype(BF16)

        rows = ROWS if final else UNROLL

        def step(i, _, lo=lo, hi=hi, row=row, rows=rows):
            first = jnp.minimum(lo + i * rows, hi - rows)
            for u in range(rows):
                row(first + u)
            return 0

        if final:
            step(0, 0)
        else:
            lax.fori_loop(0, lax.div(hi - lo + rows - 1, rows), step, 0)
        src, dst = dst, src


def weights_kernel(w_ref, bias_ref, o_ref):
    row = lax.broadcasted_iota(jnp.int32, (CH, CH), 0)
    col = lax.broadcasted_iota(jnp.int32, (CH, CH), 1)
    lane = lax.broadcasted_iota(jnp.int32, (CH, KDIM - 3 * CH), 1)
    for layer in range(LAYERS):
        bias = jnp.broadcast_to(bias_ref[layer : layer + 1, :].astype(F32) * 0.5, (CH, CH))
        column = jnp.sum(jnp.where(row == col, bias, 0.0), axis=1, keepdims=True)
        extra = jnp.where(lane == 0, column, 0.0).astype(BF16)
        none = jnp.zeros((CH, KDIM - 3 * CH), BF16)
        for b in range(3):
            taps = jnp.concatenate([w_ref[layer, a, b] for a in range(3)], axis=1)
            o_ref[layer, b * CH : (b + 1) * CH, 0 : 3 * CH] = (taps.astype(F32) * 0.5).astype(BF16)
            o_ref[layer, b * CH : (b + 1) * CH, 3 * CH :] = extra if b == 1 else none


def first_kernel(row_count, dil_ref, w_ref, xt_ref, a_ref, b_ref, c_ref, d_ref, e_ref,
                 x_ref, m0, m1, m2, m3, xa, xb, flat, turned):
    r, c, core = place()
    mask = assemble(xa, xt_ref, a_ref, b_ref, c_ref, d_ref, e_ref, c, core)

    def last(h, new):
        rounded = new.astype(BF16)
        x_ref[h] = rounded
        flat[pl.ds(h, CH, stride=ROWS), :] = rounded.astype(F32)

    run_layers(0, dil_ref, w_ref, xa, xb, mask, last, row_count)
    for g in range(16):
        four = jnp.concatenate([flat[(16 * k + g) * ROWS : (16 * k + g + 1) * ROWS, :] for k in range(4)], axis=0)
        turned[pl.ds(g, COLS, stride=16), :] = four.T
    rr = lax.rem(r, 4)
    for k, ref in enumerate((m0, m1, m2, m3)):
        start = pl.multiple_of(jnp.bitwise_xor(rr, k) * (ROWS * 16), ROWS * 16)
        ref[...] = turned[pl.ds(start, ROWS * 16), :].reshape(ROWS, 16, COLS).astype(BF16)


def mirror_kernel(x_ref, own, m0, m1, m2, m3, xt_ref, a_ref, b_ref, c_ref, got):
    r, c, core = place()
    rr = lax.rem(r, 4)
    for k, ref in enumerate((m0, m1, m2, m3)):
        got[jnp.bitwise_xor(rr, k)] = ref[...]

    @pl.when(r // 4 == c)
    def _():
        got[rr] = own[...]

    slot = lax.broadcasted_iota(jnp.int32, (16, COLS), 1) // SLOT

    def by_slot(pieces):
        out = pieces[0]
        for q in range(1, 4):
            out = jnp.where(slot >= q, pieces[q], out)
        return out

    for i in range(ROWS):
        parts = [got[q, i] for q in range(4)]
        moved = []
        for d in range(4):
            v = by_slot([parts[(q + d) % 4] for q in range(4)])
            moved.append(pltpu.roll(v, SLOT * d, 1) if d else v)
        mirrored = jnp.concatenate(
            [by_slot([moved[(q - k) % 4] for q in range(4)]) for k in range(4)], axis=0
        )
        xt_ref[i] = (0.5 * (x_ref[i].astype(F32) + mirrored.astype(F32))).astype(BF16)
    pack_sends(lambda i: xt_ref[i], a_ref, b_ref, c_ref, c, core)


def second_kernel(row_count, dil_ref, w_ref, xt_ref, a_ref, b_ref, c_ref, d_ref, e_ref, o_ref, xa, xb, flat):
    _, c, core = place()
    mask = assemble(xa, xt_ref, a_ref, b_ref, c_ref, d_ref, e_ref, c, core)

    def last(h, new):
        flat[pl.ds(h, CH, stride=ROWS), :] = new

    run_layers(HALF, dil_ref, w_ref, xa, xb, mask, last, row_count)
    o_ref[...] = flat[...].reshape(CH, ROWS, COLS).astype(BF16)


def kernel_call(body, outs, scratch, operands, smem=0, anywhere=0):
    vmem = pl.BlockSpec(memory_space=pltpu.VMEM)
    return pl.pallas_call(
        body,
        out_shape=[jax.ShapeDtypeStruct(shape, BF16) for shape in outs],
        in_specs=[pl.BlockSpec(memory_space=pltpu.SMEM)] * smem
        + [pl.BlockSpec(memory_space=pl.ANY)] * anywhere
        + [vmem] * (len(operands) - smem - anywhere),
        out_specs=[vmem] * len(outs),
        scratch_shapes=[pltpu.VMEM(*x) if isinstance(x, tuple) else x for x in scratch],
        compiler_params=pltpu.CompilerParams(vmem_limit_bytes=48 << 20),
    )(*operands)


SENDS = [(HALO, CH, COLS), (HALO, CH, COLS), (EDGE_GROUPS, CH, COLS)]
TILE = (ROWS, CH, COLS)


def swap_halos(sends, row_count):
    both = [(r, c) for r in range(row_count) for c in range(2)]

    def swap(x, partner):
        perm = [(2 * r + c, 2 * partner(r, c)[0] + partner(r, c)[1]) for r, c in both if 0 <= partner(r, c)[0] < row_count]
        return lax.ppermute(x, ("row", "col"), perm)

    a, b, c = sends
    chip = lambda r, c: (r ^ 1, c)
    across = lambda r, c: (r - 1 if r % 2 == 0 else r + 1, c)
    got_a, got_b, got_c = swap(a, chip), swap(b, across), swap(c, lambda r, c: (r, 1 - c))
    return got_a, got_b, got_c, swap(got_c, chip), swap(got_c, across)


def swap_mirror(blocks, row_count):
    both = [(r, c) for r in range(row_count) for c in range(2)]
    near = [(r, c) for r, c in both if r // 4 == c]
    far = [(r, c) for r, c in both if r // 4 != c]

    def send(x, sources, target):
        return lax.ppermute(x, ("row", "col"), [(2 * r + c, 2 * target(r, c)[0] + target(r, c)[1]) for r, c in sources])

    crossed = send(blocks[0], far, lambda r, c: (r, 1 - c))
    out = [send(blocks[k], both, lambda r, c, k=k: (4 * c + ((r % 4) ^ k), r // 4)) for k in range(1, 4)]
    return [send(crossed, near, lambda r, c: (r ^ 4, c)), *out]


def on_tile(row_count, maps, weights, biases, dilations):
    (matrices,) = kernel_call(weights_kernel, [(LAYERS, 3 * CH, KDIM)], [], [weights, biases])
    tile, *sends = kernel_call(
        pack_kernel,
        [TILE] + SENDS,
        [((CH, ROWS, COLS), BF16), ((CH * ROWS, COLS), F32), pltpu.SemaphoreType.DMA((CH // CHUNK,))],
        [maps],
        anywhere=1,
    )
    halos = swap_halos(sends, row_count)
    work = [((FULL, CH, 2 * COLS), BF16)] * 2 + [((CH * ROWS, COLS), F32)]
    tile, *blocks = kernel_call(
        functools.partial(first_kernel, row_count),
        [TILE] + [(ROWS, 16, COLS)] * 4,
        work + [((COLS * 16, COLS), F32)],
        [dilations, matrices, tile, *halos],
        smem=1,
    )
    mirrored = swap_mirror(blocks, row_count)
    tile, *sends = kernel_call(
        mirror_kernel, [TILE] + SENDS, [((4, ROWS, 16, COLS), BF16)], [tile, blocks[0], *mirrored]
    )
    halos = swap_halos(sends, row_count)
    (out,) = kernel_call(
        functools.partial(second_kernel, row_count),
        [(CH, ROWS, COLS)],
        work,
        [dilations, matrices, tile, *halos],
        smem=1,
    )
    return out


def solution(mesh):
    def step(maps, weights, biases, dilations):
        sizes = mesh.shape
        tiled = (
            sizes["ch"] == 1
            and sizes["col"] == 2
            and sizes["row"] == 8
            and maps.shape == (CH, ROWS * sizes["row"] * sizes["grp"], COLS * 2)
        )
        body = functools.partial(on_tile, sizes["row"]) if tiled else on_device
        return jax.shard_map(
            body,
            mesh=mesh,
            in_specs=(
                P("ch", ("grp", "row"), "col"),
                P(None, None, None, "ch", None),
                P(None, "ch"),
                P(),
            ),
            out_specs=P("ch", ("grp", "row"), "col"),
            check_vma=False,
        )(maps, weights, biases, dilations)

    return step
```

```python
import functools

import jax
import jax.numpy as jnp
from jax import lax
from jax.experimental import pallas as pl
from jax.experimental.pallas import tpu as pltpu
from jax.sharding import PartitionSpec as P

LAYERS = 6
DMAX = 8


def extended(block, sides, width):
    for axis, dim in sides:
        count = lax.axis_size(axis)
        forward = [(i, i + 1) for i in range(count - 1)]
        backward = [(target, source) for source, target in forward]
        low = lax.ppermute(
            lax.slice_in_dim(block, block.shape[dim] - width, None, axis=dim), axis, forward
        )
        high = lax.ppermute(lax.slice_in_dim(block, 0, width, axis=dim), axis, backward)
        block = jnp.concatenate([low, block, high], axis=dim)
    return block


def contribution(piece, weight_piece, spacing, row_count, col_count):
    count = piece.shape[0]
    out_count = weight_piece.shape[2]
    matrix = jnp.transpose(weight_piece, (2, 0, 1, 3)).reshape(out_count, 9 * count)
    block = 128
    results = []
    for block_index in range(col_count // block):
        windows = []
        for tap_row in range(3):
            for tap_col in range(3):
                row_start = DMAX + (tap_row - 1) * spacing
                col_start = DMAX + (tap_col - 1) * spacing + block_index * block
                windows.append(
                    lax.dynamic_slice(
                        piece, (jnp.int32(0), row_start, col_start), (count, row_count, block)
                    )
                )
        stacked = jnp.stack(windows, 0).reshape(9 * count, row_count * block)
        product = jnp.dot(matrix, stacked, preferred_element_type=jnp.float32)
        results.append(product.reshape(out_count, row_count, block))
    return jnp.concatenate(results, axis=2)


def finish(current, summed, tap_bias):
    branch = jax.nn.gelu(summed + tap_bias[:, None, None].astype(jnp.float32), approximate=False)
    return (current.astype(jnp.float32) + branch).astype(jnp.bfloat16)


def conv_whole(current, padded, tap_weights, tap_bias, spacing):
    summed = contribution(padded, tap_weights, spacing, current.shape[1], current.shape[2])
    return finish(current, summed, tap_bias)


def to_slab(current):
    return lax.all_to_all(current, "col", split_axis=1, concat_axis=2, tiled=True)


def to_tile(current):
    return lax.all_to_all(current, "col", split_axis=2, concat_axis=1, tiled=True)


def split_rows(current):
    return lax.all_to_all(current, "ch", split_axis=1, concat_axis=0, tiled=True)


def join_rows(current):
    return lax.all_to_all(current, "ch", split_axis=0, concat_axis=1, tiled=True)


def mirror(slab):
    flipped = jnp.swapaxes(slab, 1, 2)
    other = lax.all_to_all(flipped, ("row", "col"), split_axis=1, concat_axis=2, tiled=True)
    return (0.5 * (slab.astype(jnp.float32) + other.astype(jnp.float32))).astype(jnp.bfloat16)


def on_device(maps, weights, biases, dilations):
    layers_n = weights.shape[0]
    bias_block = biases.reshape(layers_n, 1, 1, biases.shape[1], 1)
    full_weights, full_bias = (
        lax.all_gather(weights, "ch", axis=3, tiled=True),
        lax.all_gather(bias_block, "ch", axis=3, tiled=True),
    )
    full_bias = full_bias.reshape(layers_n, full_bias.shape[3])
    current = split_rows(maps)
    for layer in range(LAYERS):
        padded = extended(current, ((("row", "ch"), 1), ("col", 2)), DMAX)
        current = conv_whole(
            current, padded, full_weights[layer], full_bias[layer], dilations[layer]
        )
        if layer == LAYERS // 2 - 1:
            current = split_rows(to_tile(mirror(to_slab(join_rows(current)))))
    return join_rows(current)


CH = 64
ROWS = 32
COLS = 128
HALF = LAYERS // 2
HALO = HALF * DMAX
EDGE_SLOTS = COLS // HALO
SLOT = 32
FULL = ROWS + 2 * HALO
KDIM = 3 * CH + 16
UNROLL = 24
BF16 = jnp.bfloat16
F32 = jnp.float32


def place():
    r, c = lax.axis_index("row"), lax.axis_index("col")
    return r, c, lax.rem(r, 2)


EDGE_GROUPS = -(-ROWS // EDGE_SLOTS)


def pack_sends(read, a_ref, b_ref, c_ref, c, core):
    off_a = (ROWS - HALO) * (1 - core)
    off_b = (ROWS - HALO) * core
    for i in range(HALO):
        a_ref[i] = read(off_a + i)
        b_ref[i] = read(off_b + i)
    lane = lax.broadcasted_iota(jnp.int32, (CH, COLS), 1)
    for t in range(EDGE_GROUPS):
        acc = None
        for q in range(EDGE_SLOTS):
            i = t + EDGE_GROUPS * q
            if i < ROWS:
                piece = pltpu.roll(read(i), lax.rem(HALO * (q + 1 - c) + c * COLS, COLS), 1)
                acc = piece if acc is None else jnp.where(lane >= HALO * q, piece, acc)
        c_ref[t] = acc


def pack_kernel(x_ref, xt_ref, a_ref, b_ref, c_ref, flat):
    _, c, core = place()
    flat[...] = x_ref[...].reshape(CH * ROWS, COLS).astype(F32)
    for h in range(ROWS):
        xt_ref[h] = flat[pl.ds(h, CH, stride=ROWS), :].astype(BF16)
    pack_sends(lambda i: xt_ref[i], a_ref, b_ref, c_ref, c, core)


def assemble(xa, xt_ref, a_ref, b_ref, c_ref, d_ref, e_ref, c, core):
    lane = lax.broadcasted_iota(jnp.int32, (CH, COLS), 1)
    first = c * (COLS - HALO)
    mask = (lane >= first) & (lane < first + HALO)
    at_a = (FULL - HALO) * (1 - core)
    at_b = (FULL - HALO) * core
    for i in range(ROWS):
        xa[HALO + i, :, 0:COLS] = xt_ref[i]
    for i in range(HALO):
        xa[at_a + i, :, 0:COLS] = a_ref[i]
        xa[at_b + i, :, 0:COLS] = b_ref[i]
    nil = jnp.zeros((CH, COLS), BF16)
    other = ROWS - HALO
    for ref, start, skip, rows in ((c_ref, HALO, 0, ROWS), (d_ref, at_a, other * core, HALO), (e_ref, at_b, other * (1 - core), HALO)):
        for i in range(rows):
            t, q = lax.rem(i + skip, EDGE_GROUPS), lax.div(i + skip, EDGE_GROUPS)
            piece = pltpu.roll(ref[t], lax.rem(COLS + first - HALO * q, COLS), 1)
            xa[start + i, :, COLS:] = jnp.where(mask, piece, nil)
    return mask


def run_layers(base, dil_ref, w_ref, xa, xb, mask, last, row_count):
    r, _, _ = place()
    lo_map = jnp.where(r == 0, HALO, 0)
    hi_map = jnp.where(r == row_count - 1, HALO + ROWS, FULL)
    lane = lax.broadcasted_iota(jnp.int32, (CH, COLS), 1)
    ones = jnp.where(lax.broadcasted_iota(jnp.int32, (16, 2 * COLS), 0) == 0, 1.0, 0.0).astype(BF16)
    zeros = jnp.zeros((CH, 2 * COLS), BF16)
    for i in range(HALO):
        xb[i] = zeros
        xb[FULL - HALO + i] = zeros
    src, dst = xa, xb
    for layer in range(HALF):
        s = dil_ref[base + layer]
        rest = 0
        for later in range(layer + 1, HALF):
            rest = rest + dil_ref[base + later]
        final = layer == HALF - 1
        lo = jnp.maximum(HALO - rest, lo_map) if not final else jnp.int32(HALO)
        hi = jnp.minimum(HALO + ROWS + rest, hi_map) if not final else jnp.int32(HALO + ROWS)
        from_left, from_right = lane >= s, lane < COLS - s

        def row(h, src=src, dst=dst, s=s, layer=layer, fl=from_left, fr=from_right, final=final):
            taps = jnp.concatenate([src[h - s], src[h], src[h + s], ones], axis=0)
            y = jnp.dot(w_ref[base + layer], taps, preferred_element_type=F32)
            left = [pltpu.roll(y[0:CH, k * COLS : (k + 1) * COLS], s, 1) for k in range(2)]
            right = [pltpu.roll(y[2 * CH :, k * COLS : (k + 1) * COLS], COLS - s, 1) for k in range(2)]
            for k in range(1 if final else 2):
                half = (
                    y[CH : 2 * CH, k * COLS : (k + 1) * COLS]
                    + jnp.where(fl, left[k], left[1 - k])
                    + jnp.where(fr, right[k], right[1 - k])
                )
                branch = half + half * lax.erf(half * 1.4142135623730951)
                new = src[h, :, k * COLS : (k + 1) * COLS].astype(F32) + branch
                if final:
                    last(h - HALO, new)
                elif k == 0:
                    dst[h, :, 0:COLS] = new.astype(BF16)
                else:
                    dst[h, :, COLS:] = jnp.where(mask, new, 0.0).astype(BF16)

        if final:
            for u in range(ROWS):
                row(lo + u)
        else:
            count = hi - lo
            for rows, fits in ((UNROLL, count <= 2 * UNROLL), (ROWS, count > 2 * UNROLL)):

                def step(i, _, lo=lo, hi=hi, row=row, rows=rows):
                    first = jnp.minimum(lo + i * rows, hi - rows)
                    for u in range(rows):
                        row(first + u)
                    return 0

                if rows == UNROLL or layer == 0:
                    lax.fori_loop(0, jnp.where(fits, lax.div(count + rows - 1, rows), 0), step, 0)
        src, dst = dst, src


def weights_kernel(w_ref, bias_ref, o_ref):
    row = lax.broadcasted_iota(jnp.int32, (CH, CH), 0)
    col = lax.broadcasted_iota(jnp.int32, (CH, CH), 1)
    lane = lax.broadcasted_iota(jnp.int32, (CH, KDIM - 3 * CH), 1)
    for layer in range(LAYERS):
        bias = jnp.broadcast_to(bias_ref[layer : layer + 1, :].astype(F32) * 0.5, (CH, CH))
        column = jnp.sum(jnp.where(row == col, bias, 0.0), axis=1, keepdims=True)
        extra = jnp.where(lane == 0, column, 0.0).astype(BF16)
        none = jnp.zeros((CH, KDIM - 3 * CH), BF16)
        for b in range(3):
            taps = jnp.concatenate([w_ref[layer, a, b] for a in range(3)], axis=1)
            o_ref[layer, b * CH : (b + 1) * CH, 0 : 3 * CH] = (taps.astype(F32) * 0.5).astype(BF16)
            o_ref[layer, b * CH : (b + 1) * CH, 3 * CH :] = extra if b == 1 else none


def first_kernel(row_count, dil_ref, w_ref, xt_ref, a_ref, b_ref, c_ref, d_ref, e_ref,
                 x_ref, m0, m1, m2, m3, xa, xb, flat, turned):
    r, c, core = place()
    mask = assemble(xa, xt_ref, a_ref, b_ref, c_ref, d_ref, e_ref, c, core)

    def last(h, new):
        rounded = new.astype(BF16)
        x_ref[h] = rounded
        flat[pl.ds(h, CH, stride=ROWS), :] = rounded.astype(F32)

    run_layers(0, dil_ref, w_ref, xa, xb, mask, last, row_count)
    for g in range(16):
        four = jnp.concatenate([flat[(16 * k + g) * ROWS : (16 * k + g + 1) * ROWS, :] for k in range(4)], axis=0)
        turned[pl.ds(g, COLS, stride=16), :] = four.T
    rr = lax.rem(r, 4)
    for k, ref in enumerate((m0, m1, m2, m3)):
        start = pl.multiple_of(jnp.bitwise_xor(rr, k) * (ROWS * 16), ROWS * 16)
        ref[...] = turned[pl.ds(start, ROWS * 16), :].reshape(ROWS, 16, COLS).astype(BF16)


def mirror_kernel(x_ref, own, m0, m1, m2, m3, xt_ref, a_ref, b_ref, c_ref, got):
    r, c, core = place()
    rr = lax.rem(r, 4)
    for k, ref in enumerate((m0, m1, m2, m3)):
        got[jnp.bitwise_xor(rr, k)] = ref[...]

    @pl.when(r // 4 == c)
    def _():
        got[rr] = own[...]

    slot = lax.broadcasted_iota(jnp.int32, (16, COLS), 1) // SLOT

    def by_slot(pieces):
        out = pieces[0]
        for q in range(1, 4):
            out = jnp.where(slot >= q, pieces[q], out)
        return out

    for i in range(ROWS):
        parts = [got[q, i] for q in range(4)]
        moved = []
        for d in range(4):
            v = by_slot([parts[(q + d) % 4] for q in range(4)])
            moved.append(pltpu.roll(v, SLOT * d, 1) if d else v)
        mirrored = jnp.concatenate(
            [by_slot([moved[(q - k) % 4] for q in range(4)]) for k in range(4)], axis=0
        )
        xt_ref[i] = (0.5 * (x_ref[i].astype(F32) + mirrored.astype(F32))).astype(BF16)
    pack_sends(lambda i: xt_ref[i], a_ref, b_ref, c_ref, c, core)


def second_kernel(row_count, dil_ref, w_ref, xt_ref, a_ref, b_ref, c_ref, d_ref, e_ref, o_ref, xa, xb, flat):
    _, c, core = place()
    mask = assemble(xa, xt_ref, a_ref, b_ref, c_ref, d_ref, e_ref, c, core)

    def last(h, new):
        flat[pl.ds(h, CH, stride=ROWS), :] = new

    run_layers(HALF, dil_ref, w_ref, xa, xb, mask, last, row_count)
    o_ref[...] = flat[...].reshape(CH, ROWS, COLS).astype(BF16)


def kernel_call(body, outs, scratch, operands, smem=0):
    vmem = pl.BlockSpec(memory_space=pltpu.VMEM)
    return pl.pallas_call(
        body,
        out_shape=[jax.ShapeDtypeStruct(shape, BF16) for shape in outs],
        in_specs=[pl.BlockSpec(memory_space=pltpu.SMEM)] * smem + [vmem] * (len(operands) - smem),
        out_specs=[vmem] * len(outs),
        scratch_shapes=[pltpu.VMEM(shape, dtype) for shape, dtype in scratch],
        compiler_params=pltpu.CompilerParams(vmem_limit_bytes=48 << 20),
    )(*operands)


SENDS = [(HALO, CH, COLS), (HALO, CH, COLS), (EDGE_GROUPS, CH, COLS)]
TILE = (ROWS, CH, COLS)


def swap_halos(sends, row_count):
    both = [(r, c) for r in range(row_count) for c in range(2)]

    def swap(x, partner):
        perm = [(2 * r + c, 2 * partner(r, c)[0] + partner(r, c)[1]) for r, c in both if 0 <= partner(r, c)[0] < row_count]
        return lax.ppermute(x, ("row", "col"), perm)

    a, b, c = sends
    chip = lambda r, c: (r ^ 1, c)
    across = lambda r, c: (r - 1 if r % 2 == 0 else r + 1, c)
    got_a, got_b, got_c = swap(a, chip), swap(b, across), swap(c, lambda r, c: (r, 1 - c))
    return got_a, got_b, got_c, swap(got_c, chip), swap(got_c, across)


def swap_mirror(blocks, row_count):
    both = [(r, c) for r in range(row_count) for c in range(2)]
    near = [(r, c) for r, c in both if r // 4 == c]
    far = [(r, c) for r, c in both if r // 4 != c]

    def send(x, sources, target):
        return lax.ppermute(x, ("row", "col"), [(2 * r + c, 2 * target(r, c)[0] + target(r, c)[1]) for r, c in sources])

    crossed = send(blocks[0], far, lambda r, c: (r, 1 - c))
    out = [send(blocks[k], both, lambda r, c, k=k: (4 * c + ((r % 4) ^ k), r // 4)) for k in range(1, 4)]
    return [send(crossed, near, lambda r, c: (r ^ 4, c)), *out]


def on_tile(row_count, maps, weights, biases, dilations):
    (matrices,) = kernel_call(weights_kernel, [(LAYERS, 3 * CH, KDIM)], [], [weights, biases])
    tile, *sends = kernel_call(pack_kernel, [TILE] + SENDS, [((CH * ROWS, COLS), F32)], [maps])
    halos = swap_halos(sends, row_count)
    work = [((FULL, CH, 2 * COLS), BF16)] * 2 + [((CH * ROWS, COLS), F32)]
    tile, *blocks = kernel_call(
        functools.partial(first_kernel, row_count),
        [TILE] + [(ROWS, 16, COLS)] * 4,
        work + [((COLS * 16, COLS), F32)],
        [dilations, matrices, tile, *halos],
        smem=1,
    )
    mirrored = swap_mirror(blocks, row_count)
    tile, *sends = kernel_call(
        mirror_kernel, [TILE] + SENDS, [((4, ROWS, 16, COLS), BF16)], [tile, blocks[0], *mirrored]
    )
    halos = swap_halos(sends, row_count)
    (out,) = kernel_call(
        functools.partial(second_kernel, row_count),
        [(CH, ROWS, COLS)],
        work,
        [dilations, matrices, tile, *halos],
        smem=1,
    )
    return out


def solution(mesh):
    def step(maps, weights, biases, dilations):
        sizes = mesh.shape
        tiled = (
            sizes["ch"] == 1
            and sizes["col"] == 2
            and sizes["row"] == 8
            and maps.shape == (CH, ROWS * sizes["row"] * sizes["grp"], COLS * 2)
        )
        body = functools.partial(on_tile, sizes["row"]) if tiled else on_device
        return jax.shard_map(
            body,
            mesh=mesh,
            in_specs=(
                P("ch", ("grp", "row"), "col"),
                P(None, None, None, "ch", None),
                P(None, "ch"),
                P(),
            ),
            out_specs=P("ch", ("grp", "row"), "col"),
            check_vma=False,
        )(maps, weights, biases, dilations)

    return step
```

```python
import functools

import jax
import jax.numpy as jnp
from jax import lax
from jax.experimental import pallas as pl
from jax.experimental.pallas import tpu as pltpu
from jax.sharding import PartitionSpec as P

LAYERS = 6
DMAX = 8


def extended(block, sides, width):
    for axis, dim in sides:
        count = lax.axis_size(axis)
        forward = [(i, i + 1) for i in range(count - 1)]
        backward = [(target, source) for source, target in forward]
        low = lax.ppermute(
            lax.slice_in_dim(block, block.shape[dim] - width, None, axis=dim), axis, forward
        )
        high = lax.ppermute(lax.slice_in_dim(block, 0, width, axis=dim), axis, backward)
        block = jnp.concatenate([low, block, high], axis=dim)
    return block


def contribution(piece, weight_piece, spacing, row_count, col_count):
    count = piece.shape[0]
    out_count = weight_piece.shape[2]
    matrix = jnp.transpose(weight_piece, (2, 0, 1, 3)).reshape(out_count, 9 * count)
    block = 128
    results = []
    for block_index in range(col_count // block):
        windows = []
        for tap_row in range(3):
            for tap_col in range(3):
                row_start = DMAX + (tap_row - 1) * spacing
                col_start = DMAX + (tap_col - 1) * spacing + block_index * block
                windows.append(
                    lax.dynamic_slice(
                        piece, (jnp.int32(0), row_start, col_start), (count, row_count, block)
                    )
                )
        stacked = jnp.stack(windows, 0).reshape(9 * count, row_count * block)
        product = jnp.dot(matrix, stacked, preferred_element_type=jnp.float32)
        results.append(product.reshape(out_count, row_count, block))
    return jnp.concatenate(results, axis=2)


def finish(current, summed, tap_bias):
    branch = jax.nn.gelu(summed + tap_bias[:, None, None].astype(jnp.float32), approximate=False)
    return (current.astype(jnp.float32) + branch).astype(jnp.bfloat16)


def conv_whole(current, padded, tap_weights, tap_bias, spacing):
    summed = contribution(padded, tap_weights, spacing, current.shape[1], current.shape[2])
    return finish(current, summed, tap_bias)


def to_slab(current):
    return lax.all_to_all(current, "col", split_axis=1, concat_axis=2, tiled=True)


def to_tile(current):
    return lax.all_to_all(current, "col", split_axis=2, concat_axis=1, tiled=True)


def split_rows(current):
    return lax.all_to_all(current, "ch", split_axis=1, concat_axis=0, tiled=True)


def join_rows(current):
    return lax.all_to_all(current, "ch", split_axis=0, concat_axis=1, tiled=True)


def mirror(slab):
    flipped = jnp.swapaxes(slab, 1, 2)
    other = lax.all_to_all(flipped, ("row", "col"), split_axis=1, concat_axis=2, tiled=True)
    return (0.5 * (slab.astype(jnp.float32) + other.astype(jnp.float32))).astype(jnp.bfloat16)


def on_device(maps, weights, biases, dilations):
    layers_n = weights.shape[0]
    bias_block = biases.reshape(layers_n, 1, 1, biases.shape[1], 1)
    full_weights, full_bias = (
        lax.all_gather(weights, "ch", axis=3, tiled=True),
        lax.all_gather(bias_block, "ch", axis=3, tiled=True),
    )
    full_bias = full_bias.reshape(layers_n, full_bias.shape[3])
    current = split_rows(maps)
    for layer in range(LAYERS):
        padded = extended(current, ((("row", "ch"), 1), ("col", 2)), DMAX)
        current = conv_whole(
            current, padded, full_weights[layer], full_bias[layer], dilations[layer]
        )
        if layer == LAYERS // 2 - 1:
            current = split_rows(to_tile(mirror(to_slab(join_rows(current)))))
    return join_rows(current)


CH = 64
ROWS = 32
COLS = 128
HALF = LAYERS // 2
HALO = HALF * DMAX
EDGE_SLOTS = COLS // HALO
SLOT = 32
FULL = ROWS + 2 * HALO
KDIM = 3 * CH + 16
UNROLL = 24
BF16 = jnp.bfloat16
F32 = jnp.float32


def place():
    r, c = lax.axis_index("row"), lax.axis_index("col")
    return r, c, lax.rem(r, 2)


EDGE_GROUPS = -(-ROWS // EDGE_SLOTS)


def pack_sends(read, a_ref, b_ref, c_ref, c, core):
    off_a = (ROWS - HALO) * (1 - core)
    off_b = (ROWS - HALO) * core
    for i in range(HALO):
        a_ref[i] = read(off_a + i)
        b_ref[i] = read(off_b + i)
    lane = lax.broadcasted_iota(jnp.int32, (CH, COLS), 1)
    for t in range(EDGE_GROUPS):
        acc = None
        for q in range(EDGE_SLOTS):
            i = t + EDGE_GROUPS * q
            if i < ROWS:
                piece = pltpu.roll(read(i), lax.rem(HALO * (q + 1 - c) + c * COLS, COLS), 1)
                acc = piece if acc is None else jnp.where(lane >= HALO * q, piece, acc)
        c_ref[t] = acc


def pack_kernel(x_ref, xt_ref, a_ref, b_ref, c_ref, flat):
    _, c, core = place()
    flat[...] = x_ref[...].reshape(CH * ROWS, COLS).astype(F32)
    for h in range(ROWS):
        xt_ref[h] = flat[pl.ds(h, CH, stride=ROWS), :].astype(BF16)
    pack_sends(lambda i: xt_ref[i], a_ref, b_ref, c_ref, c, core)


def assemble(xa, xt_ref, a_ref, b_ref, c_ref, d_ref, e_ref, c, core):
    lane = lax.broadcasted_iota(jnp.int32, (CH, COLS), 1)
    first = c * (COLS - HALO)
    mask = (lane >= first) & (lane < first + HALO)
    at_a = (FULL - HALO) * (1 - core)
    at_b = (FULL - HALO) * core
    for i in range(ROWS):
        xa[HALO + i, :, 0:COLS] = xt_ref[i]
    for i in range(HALO):
        xa[at_a + i, :, 0:COLS] = a_ref[i]
        xa[at_b + i, :, 0:COLS] = b_ref[i]
    nil = jnp.zeros((CH, COLS), BF16)
    other = ROWS - HALO
    for ref, start, skip, rows in ((c_ref, HALO, 0, ROWS), (d_ref, at_a, other * core, HALO), (e_ref, at_b, other * (1 - core), HALO)):
        for i in range(rows):
            t, q = lax.rem(i + skip, EDGE_GROUPS), lax.div(i + skip, EDGE_GROUPS)
            piece = pltpu.roll(ref[t], lax.rem(COLS + first - HALO * q, COLS), 1)
            xa[start + i, :, COLS:] = jnp.where(mask, piece, nil)
    return mask


def run_layers(base, dil_ref, w_ref, xa, xb, mask, last, row_count):
    r, _, _ = place()
    lo_map = jnp.where(r == 0, HALO, 0)
    hi_map = jnp.where(r == row_count - 1, HALO + ROWS, FULL)
    lane = lax.broadcasted_iota(jnp.int32, (CH, COLS), 1)
    ones = jnp.where(lax.broadcasted_iota(jnp.int32, (16, 2 * COLS), 0) == 0, 1.0, 0.0).astype(BF16)
    zeros = jnp.zeros((CH, 2 * COLS), BF16)

    @pl.when(r == 0)
    def _():
        for i in range(HALO):
            xb[i] = zeros

    @pl.when(r == row_count - 1)
    def _():
        for i in range(HALO):
            xb[FULL - HALO + i] = zeros

    src, dst = xa, xb
    for layer in range(HALF):
        s = dil_ref[base + layer]
        rest = 0
        for later in range(layer + 1, HALF):
            rest = rest + dil_ref[base + later]
        final = layer == HALF - 1
        lo = jnp.maximum(HALO - rest, lo_map) if not final else jnp.int32(HALO)
        hi = jnp.minimum(HALO + ROWS + rest, hi_map) if not final else jnp.int32(HALO + ROWS)
        from_left, from_right = lane >= s, lane < COLS - s

        def row(h, src=src, dst=dst, s=s, layer=layer, fl=from_left, fr=from_right, final=final):
            taps = jnp.concatenate([src[h - s], src[h], src[h + s], ones], axis=0)
            y = jnp.dot(w_ref[base + layer], taps, preferred_element_type=F32)
            left = [pltpu.roll(y[0:CH, k * COLS : (k + 1) * COLS], s, 1) for k in range(2)]
            right = [pltpu.roll(y[2 * CH :, k * COLS : (k + 1) * COLS], COLS - s, 1) for k in range(2)]
            for k in range(1 if final else 2):
                half = (
                    y[CH : 2 * CH, k * COLS : (k + 1) * COLS]
                    + jnp.where(fl, left[k], left[1 - k])
                    + jnp.where(fr, right[k], right[1 - k])
                )
                branch = half + half * lax.erf(half * 1.4142135623730951)
                new = src[h, :, k * COLS : (k + 1) * COLS].astype(F32) + branch
                if final:
                    last(h - HALO, new)
                elif k == 0:
                    dst[h, :, 0:COLS] = new.astype(BF16)
                else:
                    dst[h, :, COLS:] = jnp.where(mask, new, 0.0).astype(BF16)

        if final:
            for u in range(ROWS):
                row(lo + u)
        else:
            count = hi - lo
            for rows, fits in ((UNROLL, count <= 2 * UNROLL), (ROWS, count > 2 * UNROLL)):

                def step(i, _, lo=lo, hi=hi, row=row, rows=rows):
                    first = jnp.minimum(lo + i * rows, hi - rows)
                    for u in range(rows):
                        row(first + u)
                    return 0

                if rows == UNROLL or layer == 0:
                    lax.fori_loop(0, jnp.where(fits, lax.div(count + rows - 1, rows), 0), step, 0)
        src, dst = dst, src


def weights_kernel(w_ref, bias_ref, o_ref):
    row = lax.broadcasted_iota(jnp.int32, (CH, CH), 0)
    col = lax.broadcasted_iota(jnp.int32, (CH, CH), 1)
    lane = lax.broadcasted_iota(jnp.int32, (CH, KDIM - 3 * CH), 1)
    for layer in range(LAYERS):
        bias = jnp.broadcast_to(bias_ref[layer : layer + 1, :].astype(F32) * 0.5, (CH, CH))
        column = jnp.sum(jnp.where(row == col, bias, 0.0), axis=1, keepdims=True)
        extra = jnp.where(lane == 0, column, 0.0).astype(BF16)
        none = jnp.zeros((CH, KDIM - 3 * CH), BF16)
        for b in range(3):
            taps = jnp.concatenate([w_ref[layer, a, b] for a in range(3)], axis=1)
            o_ref[layer, b * CH : (b + 1) * CH, 0 : 3 * CH] = (taps.astype(F32) * 0.5).astype(BF16)
            o_ref[layer, b * CH : (b + 1) * CH, 3 * CH :] = extra if b == 1 else none


def first_kernel(row_count, dil_ref, w_ref, xt_ref, a_ref, b_ref, c_ref, d_ref, e_ref,
                 x_ref, m0, m1, m2, m3, xa, xb, flat, turned):
    r, c, core = place()
    mask = assemble(xa, xt_ref, a_ref, b_ref, c_ref, d_ref, e_ref, c, core)

    def last(h, new):
        rounded = new.astype(BF16)
        x_ref[h] = rounded
        flat[pl.ds(h, CH, stride=ROWS), :] = rounded.astype(F32)

    run_layers(0, dil_ref, w_ref, xa, xb, mask, last, row_count)
    for g in range(16):
        four = jnp.concatenate([flat[(16 * k + g) * ROWS : (16 * k + g + 1) * ROWS, :] for k in range(4)], axis=0)
        turned[pl.ds(g, COLS, stride=16), :] = four.T
    rr = lax.rem(r, 4)
    for k, ref in enumerate((m0, m1, m2, m3)):
        start = pl.multiple_of(jnp.bitwise_xor(rr, k) * (ROWS * 16), ROWS * 16)
        ref[...] = turned[pl.ds(start, ROWS * 16), :].reshape(ROWS, 16, COLS).astype(BF16)


def mirror_kernel(x_ref, own, m0, m1, m2, m3, xt_ref, a_ref, b_ref, c_ref, got):
    r, c, core = place()
    rr = lax.rem(r, 4)
    for k, ref in enumerate((m0, m1, m2, m3)):
        got[jnp.bitwise_xor(rr, k)] = ref[...]

    @pl.when(r // 4 == c)
    def _():
        got[rr] = own[...]

    slot = lax.broadcasted_iota(jnp.int32, (16, COLS), 1) // SLOT

    def by_slot(pieces):
        out = pieces[0]
        for q in range(1, 4):
            out = jnp.where(slot >= q, pieces[q], out)
        return out

    for i in range(ROWS):
        parts = [got[q, i] for q in range(4)]
        moved = []
        for d in range(4):
            v = by_slot([parts[(q + d) % 4] for q in range(4)])
            moved.append(pltpu.roll(v, SLOT * d, 1) if d else v)
        mirrored = jnp.concatenate(
            [by_slot([moved[(q - k) % 4] for q in range(4)]) for k in range(4)], axis=0
        )
        xt_ref[i] = (0.5 * (x_ref[i].astype(F32) + mirrored.astype(F32))).astype(BF16)
    pack_sends(lambda i: xt_ref[i], a_ref, b_ref, c_ref, c, core)


def second_kernel(row_count, dil_ref, w_ref, xt_ref, a_ref, b_ref, c_ref, d_ref, e_ref, o_ref, xa, xb, flat):
    _, c, core = place()
    mask = assemble(xa, xt_ref, a_ref, b_ref, c_ref, d_ref, e_ref, c, core)

    def last(h, new):
        flat[pl.ds(h, CH, stride=ROWS), :] = new

    run_layers(HALF, dil_ref, w_ref, xa, xb, mask, last, row_count)
    o_ref[...] = flat[...].reshape(CH, ROWS, COLS).astype(BF16)


def kernel_call(body, outs, scratch, operands, smem=0):
    vmem = pl.BlockSpec(memory_space=pltpu.VMEM)
    return pl.pallas_call(
        body,
        out_shape=[jax.ShapeDtypeStruct(shape, BF16) for shape in outs],
        in_specs=[pl.BlockSpec(memory_space=pltpu.SMEM)] * smem + [vmem] * (len(operands) - smem),
        out_specs=[vmem] * len(outs),
        scratch_shapes=[pltpu.VMEM(shape, dtype) for shape, dtype in scratch],
        compiler_params=pltpu.CompilerParams(vmem_limit_bytes=48 << 20),
    )(*operands)


SENDS = [(HALO, CH, COLS), (HALO, CH, COLS), (EDGE_GROUPS, CH, COLS)]
TILE = (ROWS, CH, COLS)


def swap_halos(sends, row_count):
    both = [(r, c) for r in range(row_count) for c in range(2)]

    def swap(x, partner):
        perm = [(2 * r + c, 2 * partner(r, c)[0] + partner(r, c)[1]) for r, c in both if 0 <= partner(r, c)[0] < row_count]
        return lax.ppermute(x, ("row", "col"), perm)

    a, b, c = sends
    chip = lambda r, c: (r ^ 1, c)
    across = lambda r, c: (r - 1 if r % 2 == 0 else r + 1, c)
    got_a, got_b, got_c = swap(a, chip), swap(b, across), swap(c, lambda r, c: (r, 1 - c))
    return got_a, got_b, got_c, swap(got_c, chip), swap(got_c, across)


def swap_mirror(blocks, row_count):
    both = [(r, c) for r in range(row_count) for c in range(2)]
    near = [(r, c) for r, c in both if r // 4 == c]
    far = [(r, c) for r, c in both if r // 4 != c]

    def send(x, sources, target):
        return lax.ppermute(x, ("row", "col"), [(2 * r + c, 2 * target(r, c)[0] + target(r, c)[1]) for r, c in sources])

    crossed = send(blocks[0], far, lambda r, c: (r, 1 - c))
    out = [send(blocks[k], both, lambda r, c, k=k: (4 * c + ((r % 4) ^ k), r // 4)) for k in range(1, 4)]
    return [send(crossed, near, lambda r, c: (r ^ 4, c)), *out]


def on_tile(row_count, maps, weights, biases, dilations):
    (matrices,) = kernel_call(weights_kernel, [(LAYERS, 3 * CH, KDIM)], [], [weights, biases])
    tile, *sends = kernel_call(pack_kernel, [TILE] + SENDS, [((CH * ROWS, COLS), F32)], [maps])
    halos = swap_halos(sends, row_count)
    work = [((FULL, CH, 2 * COLS), BF16)] * 2 + [((CH * ROWS, COLS), F32)]
    tile, *blocks = kernel_call(
        functools.partial(first_kernel, row_count),
        [TILE] + [(ROWS, 16, COLS)] * 4,
        work + [((COLS * 16, COLS), F32)],
        [dilations, matrices, tile, *halos],
        smem=1,
    )
    mirrored = swap_mirror(blocks, row_count)
    tile, *sends = kernel_call(
        mirror_kernel, [TILE] + SENDS, [((4, ROWS, 16, COLS), BF16)], [tile, blocks[0], *mirrored]
    )
    halos = swap_halos(sends, row_count)
    (out,) = kernel_call(
        functools.partial(second_kernel, row_count),
        [(CH, ROWS, COLS)],
        work,
        [dilations, matrices, tile, *halos],
        smem=1,
    )
    return out


def solution(mesh):
    def step(maps, weights, biases, dilations):
        sizes = mesh.shape
        tiled = (
            sizes["ch"] == 1
            and sizes["col"] == 2
            and sizes["row"] == 8
            and maps.shape == (CH, ROWS * sizes["row"] * sizes["grp"], COLS * 2)
        )
        body = functools.partial(on_tile, sizes["row"]) if tiled else on_device
        return jax.shard_map(
            body,
            mesh=mesh,
            in_specs=(
                P("ch", ("grp", "row"), "col"),
                P(None, None, None, "ch", None),
                P(None, "ch"),
                P(),
            ),
            out_specs=P("ch", ("grp", "row"), "col"),
            check_vma=False,
        )(maps, weights, biases, dilations)

    return step
```
